32 devices in a mesh: grp: 2 (over y), seq: 16 (over z, x, core).
Axes of the slice: x: 2, y: 2, z: 4, core: 2. Of those that a mesh axis runs over, the one named last changes fastest.
Arguments:
- queries: bfloat16 [8192, 2048], P(('grp', 'seq')), parts along dimension 0, may hold values from -6 to 6
- keys: bfloat16 [8192, 2048], P(('grp', 'seq')), parts along dimension 0, may hold values from -6 to 6
- values: bfloat16 [8192, 2048], P(('grp', 'seq')), parts along dimension 0, may hold values from -6 to 6
- level_index: int32 [8192], P(('grp', 'seq')), parts along dimension 0, may hold values from 0 to 63
- level_table: float32 [64, 18, 16], replicated, may hold values from 0 to 10
- norm_gain: float32 [2048], replicated, may hold values from 0.1 to 1.9
- out_weight: bfloat16 [2048, 2048], P(None, 'seq'), may hold values from -0.125 to 0.125
Outputs:
- block_out: bfloat16 [8192, 2048], P(('grp', 'seq')), parts along dimension 0
The draws below stay inside these ranges and needn't reach their ends.
There are 2 independent parts, one for each index of `grp`. The reference program is written for one: setup_inputs(seed, part) draws one part's arguments, and reference() takes and returns one part's arrays. A program takes and returns all parts, laid end to end along the dimension named above; an argument that names none is the same for every part. Nothing has to cross between parts.
All inputs are finite; a program needn't handle non-finite values.
Results may differ from the reference program's by a relative error of at most 0.0057.
Values may be sent and summed in bfloat16 or wider, within the bound.
A program may use at most 128 MiB of HBM per device.

```python
import math
import jax
import jax.numpy as jnp
from jax import lax

H = 16
NTAB = 64
LEVELS = 18
C = 256
D = 2048
LENGTH = 4096
N_SEQ = 16


def draw_level_table(key, part):
    lowest, highest = (math.log(0.2), math.log(5.0))
    base = jax.random.uniform(key, (NTAB, LEVELS, H), jnp.float32, lowest, highest)
    level = jnp.arange(LEVELS).astype(jnp.float32)
    shrink = jnp.exp2(-0.5 * jnp.maximum(level - 1.0, 0.0))
    return jnp.exp(base) * shrink[None, :, None]


def set_ends(values, own_key, smallest, high):
    index_at = [jax.random.randint(jax.random.fold_in(own_key, axis), (), 0, length) for axis, length in enumerate(values.shape)]
    widest = values.shape.index(max(values.shape))
    neighbour = index_at[:widest] + [(index_at[widest] + 1) % values.shape[widest]] + index_at[widest + 1:]
    return values.at[tuple(index_at)].set(smallest).at[tuple(neighbour)].set(high)


def shard_levels(stream_key, dims, cuts, least, largest):
    def one(position, shards_of):
        steps = jax.random.uniform(jax.random.fold_in(jax.random.fold_in(stream_key, 6), position), (shards_of,), jnp.float32, least / len(cuts), largest / len(cuts))
        return jnp.repeat(jnp.exp(steps), dims[position] // shards_of).reshape((-1,) + (1,) * (len(dims) - position - 1))

    level = one(*cuts[0])
    for cut in cuts[1:]:
        level = level * one(*cut)
    return level


def scatter_about(stream_key, shape, scale, limit, shards=(), held_as=jnp.bfloat16):
    drawn = scale * jax.random.normal(stream_key, shape, jnp.float32)
    if shards:
        drawn = drawn * shard_levels(stream_key, shape, shards, -0.22, 0.18)
    return jnp.clip(drawn, -limit, limit).astype(held_as)


def setup_inputs(seed: int = 0, part: int = 0) -> dict:
    key_list = jax.random.split(jax.random.key(seed), 8)
    part_keys = jax.random.split(jax.random.fold_in(key_list[7], part), 8)
    return {
        "queries": scatter_about(part_keys[0], (LENGTH, D), 1.0, 6.0, ((0, 16),)),
        "keys": scatter_about(part_keys[1], (LENGTH, D), 1.0, 6.0, ((0, 16),)),
        "values": scatter_about(part_keys[2], (LENGTH, D), 1.0, 6.0, ((0, 16),)),
        "level_index": set_ends(jax.random.randint(part_keys[3], (LENGTH,), 0, NTAB), jax.random.fold_in(part_keys[3], 1), 0, NTAB - 1).astype(jnp.int32),
        "level_table": draw_level_table(jax.random.fold_in(key_list[7], 71), part),
        "norm_gain": jnp.clip(1.0 + 0.18 * jax.random.normal(key_list[5], (D,), jnp.float32), 0.1, 1.9),
        "out_weight": scatter_about(key_list[6], (D, D), D ** -0.5, 0.125, ((1, 16),)),
    }


def reference(queries, keys, values, level_index, level_table, norm_gain, out_weight):
    heads = level_table.shape[2]
    width = queries.shape[1]
    head_dim = width // heads
    blocks = N_SEQ
    stretch = C
    log_stretch = stretch.bit_length() - 1
    log_blocks = blocks.bit_length() - 1
    scale = 1.0 / math.sqrt(head_dim)
    q_all = queries.reshape(blocks, stretch, heads, head_dim)
    k_all = keys.reshape(blocks, stretch, heads, head_dim)
    v_all = values.reshape(blocks, stretch, heads, head_dim)
    states = jnp.einsum('bshe,bshf->bhef', k_all.astype(jnp.float32), v_all.astype(jnp.float32))
    group_sums = []
    for level in range(log_blocks):
        group_sums.append(states.reshape(blocks >> level, 1 << level, heads, head_dim, head_dim).sum(axis=1))
    lam_all = level_table[level_index].reshape(blocks, stretch, level_table.shape[1], heads)
    positions = jnp.arange(stretch, dtype=jnp.int32)
    level_grid = jnp.zeros((stretch, stretch), jnp.int32)
    for bit in range(log_stretch):
        level_grid = level_grid + (jnp.right_shift(positions[:, None], bit) != jnp.right_shift(positions[None, :], bit)).astype(jnp.int32)
    causal = positions[None, :] <= positions[:, None]
    gain = norm_gain.reshape(heads, 1, head_dim)

    def one_block(block):
        q_blk = jnp.transpose(lax.dynamic_index_in_dim(q_all, block, 0, keepdims=False), (1, 0, 2)).astype(jnp.float32)
        k_blk = jnp.transpose(lax.dynamic_index_in_dim(k_all, block, 0, keepdims=False), (1, 0, 2)).astype(jnp.float32)
        v_blk = jnp.transpose(lax.dynamic_index_in_dim(v_all, block, 0, keepdims=False), (1, 0, 2)).astype(jnp.float32)
        lam_heads = jnp.transpose(lax.dynamic_index_in_dim(lam_all, block, 0, keepdims=False), (2, 0, 1))
        scores = jnp.einsum('hte,hse->hts', q_blk, k_blk) * scale
        picked = jnp.take_along_axis(lam_heads, jnp.broadcast_to(level_grid[None], (heads, stretch, stretch)), axis=2)
        weighted = jnp.where(causal[None], picked * scores, 0.0).astype(jnp.bfloat16)
        local = jnp.einsum('hts,hsf->htf', weighted.astype(jnp.float32), v_blk)
        far = jnp.zeros((heads, stretch, head_dim), jnp.float32)
        for level in range(log_blocks):
            owned = jnp.right_shift(block, level) % 2 == 1
            slot = jnp.maximum(jnp.right_shift(block, level) - 1, 0).astype(jnp.int32)
            bucket = lax.dynamic_index_in_dim(group_sums[level], slot, 0, keepdims=False).astype(jnp.bfloat16)
            term = jnp.einsum('hte,hef->htf', q_blk, bucket.astype(jnp.float32))
            weight = lam_heads[:, :, log_stretch + 1 + level:log_stretch + 2 + level]
            far = far + jnp.where(owned, weight * term * scale, 0.0)
        mixed = local + far
        normed = mixed * lax.rsqrt(lax.optimization_barrier(jnp.mean(mixed * mixed, axis=2, keepdims=True)) + 1e-06) * gain
        return jnp.transpose(normed, (1, 0, 2)).reshape(stretch, width).astype(jnp.bfloat16)
    normed_all = lax.map(one_block, jnp.arange(blocks, dtype=jnp.int32)).reshape(blocks * stretch, width)
    return jnp.dot(normed_all, out_weight, preferred_element_type=jnp.float32).astype(jnp.bfloat16)
```

```python
import functools
import math

import jax
import jax.numpy as jnp
from jax import lax
from jax.experimental import pallas as pl
from jax.experimental.pallas import tpu as pltpu
from jax.sharding import PartitionSpec as P

MESH = pl.DeviceIdType.MESH
UP, DOWN, ACROSS, OTHER, CORE = range(5)
ST, XQ, B1C, ZQ, B2C, ZS, B3C = range(7)


def from_partner(block, axis, apart):
    count = lax.axis_size(axis)
    route = []
    for low in range(count):
        high = low | 1 << apart
        if high != low and high < count:
            route += [(low, high), (high, low)]
    return lax.ppermute(block, axis, route)


def plain_body(queries, keys, values, level_index, level_table, norm_gain, out_weight):
    stretch, width = queries.shape
    table_rows, level_count, heads = level_table.shape
    head_dim = width // heads
    scale = 1.0 / math.sqrt(head_dim)
    log_stretch = stretch.bit_length() - 1
    log_blocks = lax.axis_size("seq").bit_length() - 1
    rank = lax.axis_index("seq")
    q_heads = jnp.transpose(queries.reshape(stretch, heads, head_dim), (1, 0, 2))
    k_heads = jnp.transpose(keys.reshape(stretch, heads, head_dim), (1, 0, 2))
    v_heads = jnp.transpose(values.reshape(stretch, heads, head_dim), (1, 0, 2))
    selector = (level_index[:, None] == jnp.arange(table_rows, dtype=jnp.int32)[None, :]).astype(
        jnp.float32
    )
    lam = jnp.dot(
        selector,
        level_table.reshape(table_rows, level_count * heads),
        precision=lax.Precision.HIGHEST,
    )
    lam_heads = jnp.transpose(lam.reshape(stretch, level_count, heads), (2, 0, 1))
    state = jnp.einsum("hse,hsf->hef", k_heads, v_heads, preferred_element_type=jnp.float32)
    positions = jnp.arange(stretch, dtype=jnp.int32)
    level_grid = jnp.zeros((positions.shape[0], positions.shape[0]), jnp.int32)
    for bit in range(log_stretch):
        level_grid = level_grid + (
            jnp.right_shift(positions[:, None], bit) != jnp.right_shift(positions[None, :], bit)
        ).astype(jnp.int32)
    scores = (
        jnp.einsum("hte,hse->hts", q_heads, k_heads, preferred_element_type=jnp.float32) * scale
    )
    picked = jnp.zeros_like(scores)
    for level in range(log_stretch + 1):
        picked = jnp.where((level_grid == level)[None], lam_heads[:, :, level : level + 1], picked)
    weighted = jnp.where(
        (positions[None, :] <= positions[:, None])[None], picked * scores, 0.0
    ).astype(jnp.bfloat16)
    pieces = jnp.einsum("hts,hsf->htf", weighted, v_heads, preferred_element_type=jnp.float32)
    group = state
    far = jnp.zeros((heads, stretch, head_dim), jnp.float32)
    for bit in range(log_blocks):
        owned = jnp.right_shift(rank, bit) % 2 == 1
        other = from_partner(group, "seq", bit)
        bucket = other.astype(jnp.bfloat16)
        term = jnp.einsum("hte,hef->htf", q_heads, bucket, preferred_element_type=jnp.float32)
        weight = lam_heads[:, :, log_stretch + 1 + bit : log_stretch + 2 + bit]
        far = far + jnp.where(owned, weight * term * scale, 0.0)
        if bit + 1 < log_blocks:
            group = group + other
    mixed = pieces + far
    normed = (
        mixed
        * lax.rsqrt(jnp.mean(mixed * mixed, axis=2, keepdims=True) + 1e-06)
        * norm_gain.reshape(heads, 1, head_dim)
    )
    normed = jnp.transpose(normed, (1, 0, 2)).reshape(stretch, width).astype(jnp.bfloat16)
    full_weight = lax.all_gather(out_weight, "seq", axis=1, tiled=True)
    return jnp.dot(normed, full_weight, preferred_element_type=jnp.float32).astype(jnp.bfloat16)


def kernel(
    dims,
    q_hbm, k_hbm, v_hbm, idx_ref, tab_ref, gain_ref, w_hbm, out_ref,
    q, k, v, wbuf, st, st_bf, b0, b1, b2, b3, ps, ps_bf, quad, quad_bf, mixed, normed, lam,
    load_sem, w_send, w_recv, s_send, s_recv,
):
    count, ways, part = dims
    stretch, width = q.shape
    heads, table_rows, level_count = tab_ref.shape
    head_dim = width // heads
    half = heads // 2
    piece = half // 2
    scale = 1.0 / math.sqrt(head_dim)
    log_stretch = stretch.bit_length() - 1
    mid = stretch // 2
    layers = count // (2 * ways)
    rows, cols = w_hbm.shape

    y = lax.axis_index("grp")
    r = lax.axis_index("seq")
    c = lax.rem(r, 2)
    x = lax.rem(r // 2, 2)
    z = r // 4
    to_core = (y, r + 1 - 2 * c)
    to_x = (y, r + 2 - 4 * x)
    to_y = (1 - y, r)
    to_up = (y, r + 4)
    to_down = (y, r - 4)
    mine = c * half
    has_up = z < layers - 1
    has_down = z > 0

    barrier = pltpu.get_barrier_semaphore()

    def greet(device):
        pl.semaphore_signal(barrier, inc=1, device_id=device, device_id_type=MESH)

    def wait_n(n):
        pl.semaphore_wait(barrier, n)

    greet(to_core)
    greet(to_x)
    greet(to_y)
    pl.when(has_up)(lambda: greet(to_up))
    pl.when(has_down)(lambda: greet(to_down))

    def load(i, src, dst):
        return pltpu.make_async_copy(src, dst, load_sem.at[i])

    loads = [
        load(0, k_hbm, k), load(1, v_hbm, v), load(2, q_hbm, q), load(3, w_hbm, wbuf.at[r]),
    ]
    for one in loads:
        one.start()
    pl.semaphore_wait(
        barrier, 3 + jnp.where(has_up, 1, 0) + jnp.where(has_down, 1, 0)
    )

    Y, C, O = "y", "c", "o"

    def chunk_rows(which):
        if which == C:
            return pl.ds(part, rows - 2 * part)
        side = y if which == Y else 1 - y
        return pl.ds(pl.multiple_of(side * (rows - part), 128), part)

    def chunk_id(which):
        if which == C:
            return 1
        return 2 * y if which == Y else 2 * (1 - y)

    targets = {UP: to_up, DOWN: to_down, ACROSS: to_x, OTHER: to_y, CORE: to_core}

    def w_copy(shard, which, way, own=False):
        at = chunk_rows(which)
        spot = wbuf.at[shard, at]
        return pltpu.make_async_remote_copy(
            src_ref=w_hbm.at[at] if own else spot,
            dst_ref=spot,
            send_sem=w_send.at[way, shard // 2, chunk_id(which)],
            recv_sem=w_recv.at[shard, chunk_id(which)],
            device_id=targets[way],
            device_id_type=MESH,
        )

    def shard_of(zz, xx, cc):
        return zz * 4 + xx * 2 + cc

    sent = []

    def send(cond, shard, which, way, own=False):
        def go():
            w_copy(shard, which, way, own).start()

        if cond is None:
            go()
        else:
            pl.when(cond)(go)
        sent.append((cond, shard, which, way, own))

    def both(a, b):
        return b if a is None else jnp.logical_and(a, b)

    def under(cond, go):
        if cond is None:
            go()
        else:
            pl.when(cond)(go)

    def arrive(cond, shard, which, way):
        under(cond, lambda: w_copy(shard, which, way).wait_recv())

    for which in (Y, C):
        send(has_up, r, which, UP, True)
        send(has_down, r, which, DOWN, True)
    send(None, r, Y, ACROSS, True)
    for which in (Y, C, O):
        send(None, r, which, CORE, True)

    def from_line(d, side, which):
        zz = z - d if side == UP else z + d
        ok = z >= d if side == UP else z + d < layers
        shard = shard_of(jnp.where(ok, zz, z), x, c)
        arrive(ok, shard, which, side)
        send(both(ok, has_up if side == UP else has_down), shard, which, side)
        send(ok, shard, which, ACROSS)
        if which == Y:
            send(ok, shard, which, OTHER)
        send(ok, shard, which, CORE)

    def from_across(d, side, which):
        if d == 0:
            ok, zz = None, z
        else:
            ok = z >= d if side == UP else z + d < layers
            zz = jnp.where(ok, z - d if side == UP else z + d, z)
        shard = shard_of(zz, 1 - x, c)
        arrive(ok, shard, which, ACROSS)
        if which == Y:
            send(ok, shard, which, OTHER)
        send(ok, shard, which, CORE)

    def from_other(d, side, across):
        if d == 0:
            ok, zz = None, z
        else:
            ok = z >= d if side == UP else z + d < layers
            zz = jnp.where(ok, z - d if side == UP else z + d, z)
        shard = shard_of(zz, 1 - x if across else x, c)
        arrive(ok, shard, O, OTHER)
        send(ok, shard, O, CORE)

    def line(d):
        for which in (Y, C):
            for side in (UP, DOWN):
                from_line(d, side, which)

    def across(d, which):
        for side in (UP,) if d == 0 else (UP, DOWN):
            from_across(d, side, which)

    def other(d, far_side):
        for side in (UP,) if d == 0 else (UP, DOWN):
            from_other(d, side, far_side)

    s_sent = []

    def s_copy(kind, n, src, dst, to):
        return pltpu.make_async_remote_copy(
            src_ref=src, dst_ref=dst, send_sem=s_send.at[kind, n], recv_sem=s_recv.at[kind, n],
            device_id=to, device_id_type=MESH,
        )

    def s_start(cond, *args):
        under(cond, lambda: s_copy(*args).start())
        s_sent.append((cond, args))

    def heads_at(start, n):
        return pl.ds(start, n)

    def lanes(h):
        return pl.ds(pl.multiple_of(h * head_dim, head_dim), head_dim)

    loads[0].wait()
    loads[1].wait()

    def state_loop(first):
        def step(i, _):
            for u in range(2):
                h = first + i * 2 + u
                one = lax.dot_general(
                    k[:, lanes(h)], v[:, lanes(h)], (((0,), (0,)), ((), ())),
                    preferred_element_type=jnp.float32,
                )
                st[h] = one
                st_bf[h] = one.astype(jnp.bfloat16)
            return 0

        lax.fori_loop(0, half // 2, step, 0)

    state_loop(0)
    s_start(None, ST, 0, st_bf.at[pl.ds(0, half)], b0.at[pl.ds(0, half)], to_core)
    state_loop(half)
    s_start(c == 0, ST, 1, st_bf.at[pl.ds(half, half)], b0.at[pl.ds(half, half)], to_core)

    row_of = lax.broadcasted_iota(jnp.int32, (table_rows, stretch), 0)
    onehot_t = jnp.where(row_of == idx_ref[...], 1.0, 0.0)
    onehot = jnp.transpose(onehot_t, (1, 0)).astype(jnp.bfloat16)

    def lam_step(h, _):
        full = tab_ref[h]
        hi = full.astype(jnp.bfloat16)
        rest = full - hi.astype(jnp.float32)
        mi = rest.astype(jnp.bfloat16)
        lo = (rest - mi.astype(jnp.float32)).astype(jnp.bfloat16)
        total = jnp.dot(onehot, lo, preferred_element_type=jnp.float32)
        total = total + jnp.dot(onehot, mi, preferred_element_type=jnp.float32)
        total = total + jnp.dot(onehot, hi, preferred_element_type=jnp.float32)
        lam[h, :, pl.ds(0, level_count)] = total
        return 0

    lax.fori_loop(0, heads, lam_step, 0)

    ti = lax.broadcasted_iota(jnp.int32, (mid, mid), 0)
    si = lax.broadcasted_iota(jnp.int32, (mid, mid), 1)
    grid = jnp.zeros((mid, mid), jnp.int32)
    for bit in range(log_stretch - 1):
        grid = grid + jnp.where(
            jnp.right_shift(ti, bit) != jnp.right_shift(si, bit), 1, 0
        )
    grid = jnp.where(si <= ti, grid, -1)

    def local(first, last):
        loads_done = first == 0
        if loads_done:
            loads[2].wait()

        def step(i, _):
            for u in range(2):
                h = first + i * 2 + u
                qh, kh, vh = q[:, lanes(h)], k[:, lanes(h)], v[:, lanes(h)]
                s = lax.dot_general(
                    qh, kh, (((1,), (1,)), ((), ())), preferred_element_type=jnp.float32
                ) * scale
                weight = lam[h]

                def pick(w):
                    out = jnp.zeros((mid, mid), jnp.float32)
                    for level in range(log_stretch):
                        out = jnp.where(grid == level, w[:, level : level + 1], out)
                    return out

                low, high = weight[:mid], weight[mid:]
                p00 = (pick(low) * s[:mid, :mid]).astype(jnp.bfloat16)
                p10 = (high[:, log_stretch : log_stretch + 1] * s[mid:, :mid]).astype(jnp.bfloat16)
                p11 = (pick(high) * s[mid:, mid:]).astype(jnp.bfloat16)
                mixed[pl.ds(0, mid), lanes(h)] = jnp.dot(
                    p00, vh[:mid], preferred_element_type=jnp.float32
                )
                mixed[pl.ds(mid, mid), lanes(h)] = jnp.dot(
                    jnp.concatenate([p10, p11], axis=1), vh, preferred_element_type=jnp.float32
                )
            return 0

        lax.fori_loop(0, (last - first) // 2, step, 0)

    def far(bit, bucket):
        def step(i, _):
            for u in range(2):
                h = i * 2 + u
                term = jnp.dot(q[:, lanes(h)], bucket[h], preferred_element_type=jnp.float32)
                level = log_stretch + 1 + bit
                weight = lam[h][:, level : level + 1]
                mixed[:, lanes(h)] = mixed[:, lanes(h)] + weight * term * scale
            return 0

        lax.fori_loop(0, heads // 2, step, 0)

    def own(n):
        return pl.ds(mine + n * piece, piece)

    def chip_sum():
        pl.when(c == 0)(lambda: s_copy(ST, 0, st_bf.at[pl.ds(0, half)], b0.at[pl.ds(0, half)], to_core).wait_recv())
        pl.when(c == 1)(lambda: s_copy(ST, 1, st_bf.at[pl.ds(half, half)], b0.at[pl.ds(half, half)], to_core).wait_recv())
        for n in range(2):
            def step(i, _, n=n):
                h = n * piece + i
                one = st[mine + h] + b0[mine + h].astype(jnp.float32)
                ps[h] = one
                ps_bf[h] = one.astype(jnp.bfloat16)
                return 0

            lax.fori_loop(0, piece, step, 0)
            s_start(None, XQ, n, ps_bf.at[pl.ds(n * piece, piece)], b1.at[own(n)], to_x)

    def quad_sum():
        even = lax.rem(z, 2) == 0
        for n in range(2):
            s_copy(XQ, n, ps_bf.at[pl.ds(n * piece, piece)], b1.at[own(n)], to_x).wait_recv()
            s_start(x == 1, B1C, n, b1.at[own(n)], b1.at[own(n)], to_core)

            def step(i, _, n=n):
                h = n * piece + i
                one = ps[h] + b1[mine + h].astype(jnp.float32)
                quad[h] = one
                quad_bf[h] = one.astype(jnp.bfloat16)
                return 0

            lax.fori_loop(0, piece, step, 0)
            s_start(even, ZQ, n, quad_bf.at[pl.ds(n * piece, piece)], b2.at[own(n)], to_up)

    def layer_sum():
        odd = lax.rem(z, 2) == 1
        for n in range(2):
            at = pl.ds(n * piece, piece)
            pl.when(odd)(lambda: s_copy(ZQ, n, quad_bf.at[at], b2.at[own(n)], to_down).wait_recv())
            s_start(odd, B2C, n, b2.at[own(n)], b2.at[own(n)], to_core)

            def sums(n=n):
                def step(i, _):
                    h = n * piece + i
                    ps_bf2[h] = (quad[h] + b2[mine + h].astype(jnp.float32)).astype(jnp.bfloat16)
                    return 0

                lax.fori_loop(0, piece, step, 0)

            pl.when(z == 1)(sums)
            s_start(z == 1, ZS, n, ps_bf2.at[at], b3.at[own(n)], to_up)

    ps_bf2 = quad_bf

    def top_sum():
        for n in range(2):
            pl.when(z >= 2)(lambda: s_copy(ZS, n, b3.at[own(n)], b3.at[own(n)], to_down).wait_recv())
            s_start(z == 2, ZS, n, b3.at[own(n)], b3.at[own(n)], to_up)
            s_start(z >= 2, B3C, n, b3.at[own(n)], b3.at[own(n)], to_core)

    def theirs(n):
        return pl.ds(half - mine + n * piece, piece)

    def from_core(kind, buf):
        for n in range(2):
            s_copy(kind, n, buf.at[theirs(n)], buf.at[theirs(n)], to_core).wait_recv()

    chip_sum()
    send(None, r, C, ACROSS, True)
    local(0, 4)
    line(1)
    across(0, Y)
    quad_sum()
    local(4, 8)
    across(0, C)
    other_order = []
    layer_sum()
    local(8, 12)
    line(2)
    across(1, Y)
    other(1, False)
    local(12, 16)

    def far0():
        s_copy(ST, 0, st_bf.at[pl.ds(0, half)], b0.at[pl.ds(0, half)], to_core).wait_recv()
        far(0, b0)

    def far1():
        from_core(B1C, b1)
        far(1, b1)

    def far2():
        from_core(B2C, b2)
        far(2, b2)

    def far3():
        from_core(B3C, b3)
        far(3, b3)

    pl.when(c == 1)(far0)
    other(0, True)
    across(1, C)
    top_sum()
    pl.when(x == 1)(far1)
    line(3)
    across(2, Y)
    other(1, True)
    other(2, False)
    pl.when(lax.rem(z, 2) == 1)(far2)
    across(2, C)
    pl.when(z >= 2)(far3)

    def norm_step(i, _):
        for u in range(2):
            h = i * 2 + u
            m = mixed[:, lanes(h)]
            inv = lax.rsqrt(jnp.mean(m * m, axis=1, keepdims=True) + 1e-06)
            normed[:, lanes(h)] = (m * inv * gain_ref[:, lanes(h)]).astype(jnp.bfloat16)
        return 0

    lax.fori_loop(0, heads // 2, norm_step, 0)
    across(3, Y)
    other(2, True)
    other(3, False)
    across(3, C)
    other(3, True)
    loads[3].wait()

    def partner(j, _):
        shard = j * 2 + 1 - c
        for n, size, start in ((0, part, 0), (1, rows - 2 * part, part), (2, part, rows - part)):
            at = pl.ds(start, size)
            pltpu.make_async_remote_copy(
                src_ref=wbuf.at[shard, at], dst_ref=wbuf.at[shard, at],
                send_sem=w_send.at[CORE, j, n], recv_sem=w_recv.at[shard, n],
                device_id=to_core, device_id_type=MESH,
            ).wait_recv()
        return 0

    lax.fori_loop(0, count // 2, partner, 0)

    def project(j, _):
        both_cols = jnp.concatenate([wbuf[2 * j], wbuf[2 * j + 1]], axis=1)
        out_ref[:, pl.ds(pl.multiple_of(j * 2 * cols, 2 * cols), 2 * cols)] = jnp.dot(
            normed[...], both_cols, preferred_element_type=jnp.float32
        ).astype(jnp.bfloat16)
        return 0

    lax.fori_loop(0, count // 2, project, 0)

    for cond, shard, which, way, is_own in sent:
        under(cond, lambda: w_copy(shard, which, way, is_own).wait_send())
    for cond, args in s_sent:
        under(cond, lambda: s_copy(*args).wait_send())


def kernel_body(queries, keys, values, level_index, level_table, norm_gain, out_weight):
    stretch, width = queries.shape
    table_rows, level_count, heads = level_table.shape
    head_dim = width // heads
    rows, cols = out_weight.shape
    count = lax.axis_size("seq")
    half = heads // 2
    bf, f32 = jnp.bfloat16, jnp.float32
    part = rows * 3 // 8
    square = (head_dim, head_dim)
    any_ = pl.BlockSpec(memory_space=pl.ANY)
    vmem = pl.BlockSpec(memory_space=pltpu.VMEM)
    return pl.pallas_call(
        functools.partial(kernel, (count, 2, part)),
        out_shape=jax.ShapeDtypeStruct((stretch, width), bf),
        in_specs=[any_, any_, any_, vmem, vmem, vmem, any_],
        out_specs=vmem,
        scratch_shapes=[
            pltpu.VMEM((stretch, width), bf),
            pltpu.VMEM((stretch, width), bf),
            pltpu.VMEM((stretch, width), bf),
            pltpu.VMEM((count, rows, cols), bf),
            pltpu.VMEM((heads, *square), f32),
            pltpu.VMEM((heads, *square), bf),
            pltpu.VMEM((heads, *square), bf),
            pltpu.VMEM((heads, *square), bf),
            pltpu.VMEM((heads, *square), bf),
            pltpu.VMEM((heads, *square), bf),
            pltpu.VMEM((half, *square), f32),
            pltpu.VMEM((half, *square), bf),
            pltpu.VMEM((half, *square), f32),
            pltpu.VMEM((half, *square), bf),
            pltpu.VMEM((stretch, width), f32),
            pltpu.VMEM((stretch, width), bf),
            pltpu.VMEM((heads, stretch, 128), f32),
            pltpu.SemaphoreType.DMA((4,)),
            pltpu.SemaphoreType.DMA((5, count // 2, 3)),
            pltpu.SemaphoreType.DMA((count, 3)),
            pltpu.SemaphoreType.DMA((7, 2)),
            pltpu.SemaphoreType.DMA((7, 2)),
        ],
        compiler_params=pltpu.CompilerParams(collective_id=0, has_side_effects=True),
    )(
        queries, keys, values, level_index.reshape(1, stretch),
        jnp.transpose(level_table, (2, 0, 1)), norm_gain.reshape(1, width), out_weight,
    )


def body(queries, keys, values, level_index, level_table, norm_gain, out_weight):
    heads = level_table.shape[2]
    fits = (
        lax.axis_size("seq") == 1 << 4
        and lax.axis_size("grp") == 2
        and out_weight.shape[1] % 128 == 0
        and queries.shape[1] // heads == 128
        and heads % 4 == 0
    )
    run = kernel_body if fits else plain_body
    return run(queries, keys, values, level_index, level_table, norm_gain, out_weight)


def solution(mesh):
    placed = (
        P(("grp", "seq"), None),
        P(("grp", "seq"), None),
        P(("grp", "seq"), None),
        P(("grp", "seq")),
        P(),
        P(),
        P(None, "seq"),
    )
    return jax.shard_map(
        body, mesh=mesh, in_specs=placed, out_specs=P(("grp", "seq"), None), check_vma=False
    )
```

```python
import functools
import math

import jax
import jax.numpy as jnp
from jax import lax
from jax.experimental import pallas as pl
from jax.experimental.pallas import tpu as pltpu
from jax.sharding import PartitionSpec as P

MESH = pl.DeviceIdType.MESH
UP, DOWN, ACROSS, OTHER, CORE = range(5)
ST, XQ, B1C, ZQ, B2C, ZS, B3C = range(7)


def from_partner(block, axis, apart):
    count = lax.axis_size(axis)
    route = []
    for low in range(count):
        high = low | 1 << apart
        if high != low and high < count:
            route += [(low, high), (high, low)]
    return lax.ppermute(block, axis, route)


def plain_body(queries, keys, values, level_index, level_table, norm_gain, out_weight):
    stretch, width = queries.shape
    table_rows, level_count, heads = level_table.shape
    head_dim = width // heads
    scale = 1.0 / math.sqrt(head_dim)
    log_stretch = stretch.bit_length() - 1
    log_blocks = lax.axis_size("seq").bit_length() - 1
    rank = lax.axis_index("seq")
    q_heads = jnp.transpose(queries.reshape(stretch, heads, head_dim), (1, 0, 2))
    k_heads = jnp.transpose(keys.reshape(stretch, heads, head_dim), (1, 0, 2))
    v_heads = jnp.transpose(values.reshape(stretch, heads, head_dim), (1, 0, 2))
    selector = (level_index[:, None] == jnp.arange(table_rows, dtype=jnp.int32)[None, :]).astype(
        jnp.float32
    )
    lam = jnp.dot(
        selector,
        level_table.reshape(table_rows, level_count * heads),
        precision=lax.Precision.HIGHEST,
    )
    lam_heads = jnp.transpose(lam.reshape(stretch, level_count, heads), (2, 0, 1))
    state = jnp.einsum("hse,hsf->hef", k_heads, v_heads, preferred_element_type=jnp.float32)
    positions = jnp.arange(stretch, dtype=jnp.int32)
    level_grid = jnp.zeros((positions.shape[0], positions.shape[0]), jnp.int32)
    for bit in range(log_stretch):
        level_grid = level_grid + (
            jnp.right_shift(positions[:, None], bit) != jnp.right_shift(positions[None, :], bit)
        ).astype(jnp.int32)
    scores = (
        jnp.einsum("hte,hse->hts", q_heads, k_heads, preferred_element_type=jnp.float32) * scale
    )
    picked = jnp.zeros_like(scores)
    for level in range(log_stretch + 1):
        picked = jnp.where((level_grid == level)[None], lam_heads[:, :, level : level + 1], picked)
    weighted = jnp.where(
        (positions[None, :] <= positions[:, None])[None], picked * scores, 0.0
    ).astype(jnp.bfloat16)
    pieces = jnp.einsum("hts,hsf->htf", weighted, v_heads, preferred_element_type=jnp.float32)
    group = state
    far = jnp.zeros((heads, stretch, head_dim), jnp.float32)
    for bit in range(log_blocks):
        owned = jnp.right_shift(rank, bit) % 2 == 1
        other = from_partner(group, "seq", bit)
        bucket = other.astype(jnp.bfloat16)
        term = jnp.einsum("hte,hef->htf", q_heads, bucket, preferred_element_type=jnp.float32)
        weight = lam_heads[:, :, log_stretch + 1 + bit : log_stretch + 2 + bit]
        far = far + jnp.where(owned, weight * term * scale, 0.0)
        if bit + 1 < log_blocks:
            group = group + other
    mixed = pieces + far
    normed = (
        mixed
        * lax.rsqrt(jnp.mean(mixed * mixed, axis=2, keepdims=True) + 1e-06)
        * norm_gain.reshape(heads, 1, head_dim)
    )
    normed = jnp.transpose(normed, (1, 0, 2)).reshape(stretch, width).astype(jnp.bfloat16)
    full_weight = lax.all_gather(out_weight, "seq", axis=1, tiled=True)
    return jnp.dot(normed, full_weight, preferred_element_type=jnp.float32).astype(jnp.bfloat16)


def kernel(
    dims,
    q_hbm, k_hbm, v_hbm, idx_ref, tab_ref, gain_ref, w_hbm, out_ref,
    q, k, v, wbuf, st, st_bf, b0, b1, b2, b3, ps, ps_bf, quad, quad_bf, mixed, normed, lam,
    load_sem, w_send, w_recv, s_send, s_recv,
):
    count, ways, part = dims
    stretch, width = q.shape
    level_count, heads, table_rows = tab_ref.shape
    head_dim = width // heads
    half = heads // 2
    piece = half // 2
    scale = 1.0 / math.sqrt(head_dim)
    log_stretch = stretch.bit_length() - 1
    mid = stretch // 2
    layers = count // (2 * ways)
    rows, cols = w_hbm.shape

    y = lax.axis_index("grp")
    r = lax.axis_index("seq")
    c = lax.rem(r, 2)
    x = lax.rem(r // 2, 2)
    z = r // 4
    to_core = (y, r + 1 - 2 * c)
    to_x = (y, r + 2 - 4 * x)
    to_y = (1 - y, r)
    to_up = (y, r + 4)
    to_down = (y, r - 4)
    mine = c * half
    has_up = z < layers - 1
    has_down = z > 0

    barrier = pltpu.get_barrier_semaphore()

    def greet(device):
        pl.semaphore_signal(barrier, inc=1, device_id=device, device_id_type=MESH)

    def wait_n(n):
        pl.semaphore_wait(barrier, n)

    greet(to_core)
    greet(to_x)
    greet(to_y)
    pl.when(has_up)(lambda: greet(to_up))
    pl.when(has_down)(lambda: greet(to_down))

    def load(i, src, dst):
        return pltpu.make_async_copy(src, dst, load_sem.at[i])

    loads = [
        load(0, k_hbm, k), load(1, v_hbm, v), load(2, q_hbm, q), load(3, w_hbm, wbuf.at[r]),
    ]
    for one in loads:
        one.start()
    pl.semaphore_wait(
        barrier, 3 + jnp.where(has_up, 1, 0) + jnp.where(has_down, 1, 0)
    )

    Y, C, O = "y", "c", "o"

    def chunk_rows(which):
        if which == C:
            return pl.ds(part, rows - 2 * part)
        side = y if which == Y else 1 - y
        return pl.ds(pl.multiple_of(side * (rows - part), 128), part)

    def chunk_id(which):
        if which == C:
            return 1
        return 2 * y if which == Y else 2 * (1 - y)

    targets = {UP: to_up, DOWN: to_down, ACROSS: to_x, OTHER: to_y, CORE: to_core}

    def w_copy(shard, which, way, own=False):
        at = chunk_rows(which)
        spot = wbuf.at[shard, at]
        return pltpu.make_async_remote_copy(
            src_ref=w_hbm.at[at] if own else spot,
            dst_ref=spot,
            send_sem=w_send.at[way, shard // 2, chunk_id(which)],
            recv_sem=w_recv.at[shard, chunk_id(which)],
            device_id=targets[way],
            device_id_type=MESH,
        )

    def shard_of(zz, xx, cc):
        return zz * 4 + xx * 2 + cc

    sent = []

    def send(cond, shard, which, way, own=False):
        def go():
            w_copy(shard, which, way, own).start()

        if cond is None:
            go()
        else:
            pl.when(cond)(go)
        sent.append((cond, shard, which, way, own))

    def both(a, b):
        return b if a is None else jnp.logical_and(a, b)

    def under(cond, go):
        if cond is None:
            go()
        else:
            pl.when(cond)(go)

    def arrive(cond, shard, which, way):
        under(cond, lambda: w_copy(shard, which, way).wait_recv())

    for which in (Y, C):
        send(has_up, r, which, UP, True)
        send(has_down, r, which, DOWN, True)
    send(None, r, Y, ACROSS, True)
    for which in (Y, C, O):
        send(None, r, which, CORE, True)

    def from_line(d, side, which):
        zz = z - d if side == UP else z + d
        ok = z >= d if side == UP else z + d < layers
        shard = shard_of(jnp.where(ok, zz, z), x, c)
        arrive(ok, shard, which, side)
        send(both(ok, has_up if side == UP else has_down), shard, which, side)
        if which == Y:
            send(ok, shard, which, ACROSS)
            send(ok, shard, which, OTHER)
        send(ok, shard, which, CORE)

    def late(d):
        for side in (UP, DOWN):
            zz = z - d if side == UP else z + d
            ok = z >= d if side == UP else z + d < layers
            send(ok, shard_of(jnp.where(ok, zz, z), x, c), C, ACROSS)

    def from_across(d, side, which):
        if d == 0:
            ok, zz = None, z
        else:
            ok = z >= d if side == UP else z + d < layers
            zz = jnp.where(ok, z - d if side == UP else z + d, z)
        shard = shard_of(zz, 1 - x, c)
        arrive(ok, shard, which, ACROSS)
        if which == Y:
            send(ok, shard, which, OTHER)
        send(ok, shard, which, CORE)

    def from_other(d, side, across):
        if d == 0:
            ok, zz = None, z
        else:
            ok = z >= d if side == UP else z + d < layers
            zz = jnp.where(ok, z - d if side == UP else z + d, z)
        shard = shard_of(zz, 1 - x if across else x, c)
        arrive(ok, shard, O, OTHER)
        send(ok, shard, O, CORE)

    def line(d, which):
        for side in (UP, DOWN):
            from_line(d, side, which)

    def across(d, which):
        for side in (UP,) if d == 0 else (UP, DOWN):
            from_across(d, side, which)

    def other(d, far_side):
        for side in (UP,) if d == 0 else (UP, DOWN):
            from_other(d, side, far_side)

    s_sent = []

    def s_copy(kind, n, src, dst, to):
        return pltpu.make_async_remote_copy(
            src_ref=src, dst_ref=dst, send_sem=s_send.at[kind, n], recv_sem=s_recv.at[kind, n],
            device_id=to, device_id_type=MESH,
        )

    def s_start(cond, *args):
        under(cond, lambda: s_copy(*args).start())
        s_sent.append((cond, args))

    def heads_at(start, n):
        return pl.ds(start, n)

    def lanes(h):
        return pl.ds(pl.multiple_of(h * head_dim, head_dim), head_dim)

    loads[0].wait()
    loads[1].wait()

    def state_loop(first):
        def step(i, _):
            for u in range(2):
                h = first + i * 2 + u
                one = lax.dot_general(
                    k[:, lanes(h)], v[:, lanes(h)], (((0,), (0,)), ((), ())),
                    preferred_element_type=jnp.float32,
                )
                st[h] = one
                st_bf[h] = one.astype(jnp.bfloat16)
            return 0

        lax.fori_loop(0, half // 2, step, 0)

    state_loop(0)
    s_start(None, ST, 0, st_bf.at[pl.ds(0, half)], b0.at[pl.ds(0, half)], to_core)
    state_loop(half)
    s_start(c == 0, ST, 1, st_bf.at[pl.ds(half, half)], b0.at[pl.ds(half, half)], to_core)

    row_of = lax.broadcasted_iota(jnp.int32, (table_rows, stretch), 0)
    onehot_t = jnp.where(row_of == idx_ref[...], 1.0, 0.0)
    onehot = jnp.transpose(onehot_t, (1, 0)).astype(jnp.bfloat16)

    def lam_step(h, _):
        full = tab_ref[:, pl.ds(h, 1), :].reshape(level_count, table_rows)
        full = jnp.transpose(full, (1, 0))
        hi = full.astype(jnp.bfloat16)
        rest = full - hi.astype(jnp.float32)
        mi = rest.astype(jnp.bfloat16)
        lo = (rest - mi.astype(jnp.float32)).astype(jnp.bfloat16)
        total = jnp.dot(onehot, lo, preferred_element_type=jnp.float32)
        total = total + jnp.dot(onehot, mi, preferred_element_type=jnp.float32)
        total = total + jnp.dot(onehot, hi, preferred_element_type=jnp.float32)
        lam[h, :, pl.ds(0, level_count)] = total
        return 0

    lax.fori_loop(0, heads, lam_step, 0)

    ti = lax.broadcasted_iota(jnp.int32, (mid, mid), 0)
    si = lax.broadcasted_iota(jnp.int32, (mid, mid), 1)
    grid = jnp.zeros((mid, mid), jnp.int32)
    for bit in range(log_stretch - 1):
        grid = grid + jnp.where(
            jnp.right_shift(ti, bit) != jnp.right_shift(si, bit), 1, 0
        )
    grid = jnp.where(si <= ti, grid, -1)

    def local(first, last):
        loads_done = first == 0
        if loads_done:
            loads[2].wait()

        def step(i, _):
            for u in range(2):
                h = first + i * 2 + u
                qh, kh, vh = q[:, lanes(h)], k[:, lanes(h)], v[:, lanes(h)]
                s = lax.dot_general(
                    qh, kh, (((1,), (1,)), ((), ())), preferred_element_type=jnp.float32
                ) * scale
                weight = lam[h]

                def pick(w):
                    out = jnp.zeros((mid, mid), jnp.float32)
                    for level in range(log_stretch):
                        out = jnp.where(grid == level, w[:, level : level + 1], out)
                    return out

                low, high = weight[:mid], weight[mid:]
                p00 = (pick(low) * s[:mid, :mid]).astype(jnp.bfloat16)
                p10 = (high[:, log_stretch : log_stretch + 1] * s[mid:, :mid]).astype(jnp.bfloat16)
                p11 = (pick(high) * s[mid:, mid:]).astype(jnp.bfloat16)
                mixed[pl.ds(0, mid), lanes(h)] = jnp.dot(
                    p00, vh[:mid], preferred_element_type=jnp.float32
                )
                mixed[pl.ds(mid, mid), lanes(h)] = jnp.dot(
                    jnp.concatenate([p10, p11], axis=1), vh, preferred_element_type=jnp.float32
                )
            return 0

        lax.fori_loop(0, (last - first) // 2, step, 0)

    def far(bit, bucket):
        def step(i, _):
            for u in range(2):
                h = i * 2 + u
                term = jnp.dot(q[:, lanes(h)], bucket[h], preferred_element_type=jnp.float32)
                level = log_stretch + 1 + bit
                weight = lam[h][:, level : level + 1]
                mixed[:, lanes(h)] = mixed[:, lanes(h)] + weight * term * scale
            return 0

        lax.fori_loop(0, heads // 2, step, 0)

    def own(n):
        return pl.ds(mine + n * piece, piece)

    def chip_sum():
        pl.when(c == 0)(lambda: s_copy(ST, 0, st_bf.at[pl.ds(0, half)], b0.at[pl.ds(0, half)], to_core).wait_recv())
        pl.when(c == 1)(lambda: s_copy(ST, 1, st_bf.at[pl.ds(half, half)], b0.at[pl.ds(half, half)], to_core).wait_recv())
        for n in range(2):
            def step(i, _, n=n):
                h = n * piece + i
                one = st[mine + h] + b0[mine + h].astype(jnp.float32)
                ps[h] = one
                ps_bf[h] = one.astype(jnp.bfloat16)
                return 0

            lax.fori_loop(0, piece, step, 0)
            s_start(None, XQ, n, ps_bf.at[pl.ds(n * piece, piece)], b1.at[own(n)], to_x)

    def quad_sum():
        even = lax.rem(z, 2) == 0
        for n in range(2):
            s_copy(XQ, n, ps_bf.at[pl.ds(n * piece, piece)], b1.at[own(n)], to_x).wait_recv()
            s_start(x == 1, B1C, n, b1.at[own(n)], b1.at[own(n)], to_core)

            def step(i, _, n=n):
                h = n * piece + i
                one = ps[h] + b1[mine + h].astype(jnp.float32)
                quad[h] = one
                quad_bf[h] = one.astype(jnp.bfloat16)
                return 0

            lax.fori_loop(0, piece, step, 0)
            s_start(even, ZQ, n, quad_bf.at[pl.ds(n * piece, piece)], b2.at[own(n)], to_up)

    def layer_sum():
        odd = lax.rem(z, 2) == 1
        for n in range(2):
            at = pl.ds(n * piece, piece)
            pl.when(odd)(lambda: s_copy(ZQ, n, quad_bf.at[at], b2.at[own(n)], to_down).wait_recv())
            s_start(odd, B2C, n, b2.at[own(n)], b2.at[own(n)], to_core)

            def sums(n=n):
                def step(i, _):
                    h = n * piece + i
                    ps_bf2[h] = (quad[h] + b2[mine + h].astype(jnp.float32)).astype(jnp.bfloat16)
                    return 0

                lax.fori_loop(0, piece, step, 0)

            pl.when(z == 1)(sums)
            s_start(z == 1, ZS, n, ps_bf2.at[at], b3.at[own(n)], to_up)

    ps_bf2 = quad_bf

    def top_sum(layer):
        there = z == layer
        for n in range(2):
            def arrived(n=n):
                s_copy(ZS, n, b3.at[own(n)], b3.at[own(n)], to_down).wait_recv()

            pl.when(there)(arrived)
            if layer + 1 < layers:
                s_start(there, ZS, n, b3.at[own(n)], b3.at[own(n)], to_up)
            s_start(there, B3C, n, b3.at[own(n)], b3.at[own(n)], to_core)

    def theirs(n):
        return pl.ds(half - mine + n * piece, piece)

    def from_core(kind, buf):
        for n in range(2):
            s_copy(kind, n, buf.at[theirs(n)], buf.at[theirs(n)], to_core).wait_recv()

    def far0():
        s_copy(ST, 0, st_bf.at[pl.ds(0, half)], b0.at[pl.ds(0, half)], to_core).wait_recv()
        far(0, b0)

    def far1():
        from_core(B1C, b1)
        far(1, b1)

    def far2():
        from_core(B2C, b2)
        far(2, b2)

    def far3():
        from_core(B3C, b3)
        far(3, b3)

    def norm_step(i, _):
        for u in range(2):
            h = i * 2 + u
            m = mixed[:, lanes(h)]
            inv = lax.rsqrt(jnp.mean(m * m, axis=1, keepdims=True) + 1e-06)
            normed[:, lanes(h)] = (m * inv * gain_ref[:, lanes(h)]).astype(jnp.bfloat16)
        return 0

    def partner(column):
        def step(zz, _):
            j = zz * 2 + column
            shard = j * 2 + 1 - c
            for n, size, start in ((0, part, 0), (1, rows - 2 * part, part), (2, part, rows - part)):
                at = pl.ds(start, size)
                pltpu.make_async_remote_copy(
                    src_ref=wbuf.at[shard, at], dst_ref=wbuf.at[shard, at],
                    send_sem=w_send.at[CORE, j, n], recv_sem=w_recv.at[shard, n],
                    device_id=to_core, device_id_type=MESH,
                ).wait_recv()
            return 0

        lax.fori_loop(0, layers, step, 0)

    def project(column):
        def step(zz, _):
            j = zz * 2 + column
            both_cols = jnp.concatenate([wbuf[2 * j], wbuf[2 * j + 1]], axis=1)
            out_ref[:, pl.ds(pl.multiple_of(j * 2 * cols, 2 * cols), 2 * cols)] = jnp.dot(
                normed[...], both_cols, preferred_element_type=jnp.float32
            ).astype(jnp.bfloat16)
            return 0

        lax.fori_loop(0, layers, step, 0)

    chip_sum()
    across(0, Y)
    line(1, Y)
    local(0, 4)
    line(1, C)
    local(4, 6)
    line(2, Y)
    other(1, False)
    quad_sum()
    line(2, C)
    send(None, r, C, ACROSS, True)
    late(1)
    other(0, True)
    local(6, 8)
    line(3, Y)
    across(1, Y)
    layer_sum()
    line(3, C)
    late(2)
    late(3)
    other(2, False)
    across(2, Y)
    local(8, 12)
    top_sum(layers - 2)
    other(1, True)
    across(0, C)
    local(12, 16)
    pl.when(c == 1)(far0)
    across(1, C)
    other(3, False)
    pl.when(x == 1)(far1)
    across(3, Y)
    other(2, True)
    top_sum(layers - 1)
    pl.when(lax.rem(z, 2) == 1)(far2)
    across(2, C)
    pl.when(z >= 2)(far3)
    lax.fori_loop(0, heads // 2, norm_step, 0)
    loads[3].wait()
    partner(x)
    across(3, C)
    other(3, True)
    project(x)
    partner(1 - x)
    project(1 - x)

    for cond, shard, which, way, is_own in sent:
        under(cond, lambda: w_copy(shard, which, way, is_own).wait_send())
    for cond, args in s_sent:
        under(cond, lambda: s_copy(*args).wait_send())


def kernel_body(queries, keys, values, level_index, level_table, norm_gain, out_weight):
    stretch, width = queries.shape
    table_rows, level_count, heads = level_table.shape
    head_dim = width // heads
    rows, cols = out_weight.shape
    count = lax.axis_size("seq")
    half = heads // 2
    bf, f32 = jnp.bfloat16, jnp.float32
    part = rows * 3 // 8
    square = (head_dim, head_dim)
    any_ = pl.BlockSpec(memory_space=pl.ANY)
    vmem = pl.BlockSpec(memory_space=pltpu.VMEM)
    return pl.pallas_call(
        functools.partial(kernel, (count, 2, part)),
        out_shape=jax.ShapeDtypeStruct((stretch, width), bf),
        in_specs=[any_, any_, any_, vmem, vmem, vmem, any_],
        out_specs=vmem,
        scratch_shapes=[
            pltpu.VMEM((stretch, width), bf),
            pltpu.VMEM((stretch, width), bf),
            pltpu.VMEM((stretch, width), bf),
            pltpu.VMEM((count, rows, cols), bf),
            pltpu.VMEM((heads, *square), f32),
            pltpu.VMEM((heads, *square), bf),
            pltpu.VMEM((heads, *square), bf),
            pltpu.VMEM((heads, *square), bf),
            pltpu.VMEM((heads, *square), bf),
            pltpu.VMEM((heads, *square), bf),
            pltpu.VMEM((half, *square), f32),
            pltpu.VMEM((half, *square), bf),
            pltpu.VMEM((half, *square), f32),
            pltpu.VMEM((half, *square), bf),
            pltpu.VMEM((stretch, width), f32),
            pltpu.VMEM((stretch, width), bf),
            pltpu.VMEM((heads, stretch, 128), f32),
            pltpu.SemaphoreType.DMA((4,)),
            pltpu.SemaphoreType.DMA((5, count // 2, 3)),
            pltpu.SemaphoreType.DMA((count, 3)),
            pltpu.SemaphoreType.DMA((7, 2)),
            pltpu.SemaphoreType.DMA((7, 2)),
        ],
        compiler_params=pltpu.CompilerParams(collective_id=0, has_side_effects=True),
    )(
        queries, keys, values, level_index.reshape(1, stretch),
        jnp.transpose(level_table, (1, 2, 0)), norm_gain.reshape(1, width), out_weight,
    )


def body(queries, keys, values, level_index, level_table, norm_gain, out_weight):
    heads = level_table.shape[2]
    fits = (
        lax.axis_size("seq") == 1 << 4
        and lax.axis_size("grp") == 2
        and out_weight.shape[1] % 128 == 0
        and queries.shape[1] // heads == 128
        and heads % 4 == 0
    )
    run = kernel_body if fits else plain_body
    return run(queries, keys, values, level_index, level_table, norm_gain, out_weight)


def solution(mesh):
    placed = (
        P(("grp", "seq"), None),
        P(("grp", "seq"), None),
        P(("grp", "seq"), None),
        P(("grp", "seq")),
        P(),
        P(),
        P(None, "seq"),
    )
    return jax.shard_map(
        body, mesh=mesh, in_specs=placed, out_specs=P(("grp", "seq"), None), check_vma=False
    )
```

```python
import functools
import math

import jax
import jax.numpy as jnp
from jax import lax
from jax.experimental import pallas as pl
from jax.experimental.pallas import tpu as pltpu
from jax.sharding import PartitionSpec as P

MESH = pl.DeviceIdType.MESH
UP, DOWN, ACROSS, OTHER, CORE = range(5)
ST, XQ, B1C, ZQ, B2C, ZS, B3C = range(7)


def from_partner(block, axis, apart):
    count = lax.axis_size(axis)
    route = []
    for low in range(count):
        high = low | 1 << apart
        if high != low and high < count:
            route += [(low, high), (high, low)]
    return lax.ppermute(block, axis, route)


def plain_body(queries, keys, values, level_index, level_table, norm_gain, out_weight):
    stretch, width = queries.shape
    table_rows, level_count, heads = level_table.shape
    head_dim = width // heads
    scale = 1.0 / math.sqrt(head_dim)
    log_stretch = stretch.bit_length() - 1
    log_blocks = lax.axis_size("seq").bit_length() - 1
    rank = lax.axis_index("seq")
    q_heads = jnp.transpose(queries.reshape(stretch, heads, head_dim), (1, 0, 2))
    k_heads = jnp.transpose(keys.reshape(stretch, heads, head_dim), (1, 0, 2))
    v_heads = jnp.transpose(values.reshape(stretch, heads, head_dim), (1, 0, 2))
    selector = (level_index[:, None] == jnp.arange(table_rows, dtype=jnp.int32)[None, :]).astype(
        jnp.float32
    )
    lam = jnp.dot(
        selector,
        level_table.reshape(table_rows, level_count * heads),
        precision=lax.Precision.HIGHEST,
    )
    lam_heads = jnp.transpose(lam.reshape(stretch, level_count, heads), (2, 0, 1))
    state = jnp.einsum("hse,hsf->hef", k_heads, v_heads, preferred_element_type=jnp.float32)
    positions = jnp.arange(stretch, dtype=jnp.int32)
    level_grid = jnp.zeros((positions.shape[0], positions.shape[0]), jnp.int32)
    for bit in range(log_stretch):
        level_grid = level_grid + (
            jnp.right_shift(positions[:, None], bit) != jnp.right_shift(positions[None, :], bit)
        ).astype(jnp.int32)
    scores = (
        jnp.einsum("hte,hse->hts", q_heads, k_heads, preferred_element_type=jnp.float32) * scale
    )
    picked = jnp.zeros_like(scores)
    for level in range(log_stretch + 1):
        picked = jnp.where((level_grid == level)[None], lam_heads[:, :, level : level + 1], picked)
    weighted = jnp.where(
        (positions[None, :] <= positions[:, None])[None], picked * scores, 0.0
    ).astype(jnp.bfloat16)
    pieces = jnp.einsum("hts,hsf->htf", weighted, v_heads, preferred_element_type=jnp.float32)
    group = state
    far = jnp.zeros((heads, stretch, head_dim), jnp.float32)
    for bit in range(log_blocks):
        owned = jnp.right_shift(rank, bit) % 2 == 1
        other = from_partner(group, "seq", bit)
        bucket = other.astype(jnp.bfloat16)
        term = jnp.einsum("hte,hef->htf", q_heads, bucket, preferred_element_type=jnp.float32)
        weight = lam_heads[:, :, log_stretch + 1 + bit : log_stretch + 2 + bit]
        far = far + jnp.where(owned, weight * term * scale, 0.0)
        if bit + 1 < log_blocks:
            group = group + other
    mixed = pieces + far
    normed = (
        mixed
        * lax.rsqrt(jnp.mean(mixed * mixed, axis=2, keepdims=True) + 1e-06)
        * norm_gain.reshape(heads, 1, head_dim)
    )
    normed = jnp.transpose(normed, (1, 0, 2)).reshape(stretch, width).astype(jnp.bfloat16)
    full_weight = lax.all_gather(out_weight, "seq", axis=1, tiled=True)
    return jnp.dot(normed, full_weight, preferred_element_type=jnp.float32).astype(jnp.bfloat16)


def kernel(
    dims,
    q_hbm, k_hbm, v_hbm, idx_ref, tab_ref, gain_ref, w_hbm, out_ref,
    q, k, v, wbuf, st, st_bf, b0, b1, b2, b3, ps, ps_bf, quad, quad_bf, mixed, normed, lam,
    load_sem, w_send, w_recv, s_send, s_recv,
):
    count, ways, part = dims
    stretch, width = q.shape
    level_count, heads, table_rows = tab_ref.shape
    head_dim = width // heads
    half = heads // 2
    piece = half // 2
    scale = 1.0 / math.sqrt(head_dim)
    log_stretch = stretch.bit_length() - 1
    mid = stretch // 2
    layers = count // (2 * ways)
    rows, cols = w_hbm.shape

    y = lax.axis_index("grp")
    r = lax.axis_index("seq")
    c = lax.rem(r, 2)
    x = lax.rem(r // 2, 2)
    z = r // 4
    to_core = (y, r + 1 - 2 * c)
    to_x = (y, r + 2 - 4 * x)
    to_y = (1 - y, r)
    to_up = (y, r + 4)
    to_down = (y, r - 4)
    mine = c * half
    has_up = z < layers - 1
    has_down = z > 0

    barrier = pltpu.get_barrier_semaphore()

    def greet(device):
        pl.semaphore_signal(barrier, inc=1, device_id=device, device_id_type=MESH)

    def wait_n(n):
        pl.semaphore_wait(barrier, n)

    greet(to_core)
    greet(to_x)
    greet(to_y)
    pl.when(has_up)(lambda: greet(to_up))
    pl.when(has_down)(lambda: greet(to_down))

    def load(i, src, dst):
        return pltpu.make_async_copy(src, dst, load_sem.at[i])

    loads = [
        load(0, k_hbm, k), load(1, v_hbm, v), load(2, q_hbm, q), load(3, w_hbm, wbuf.at[r]),
    ]
    for one in loads:
        one.start()
    pl.semaphore_wait(
        barrier, 3 + jnp.where(has_up, 1, 0) + jnp.where(has_down, 1, 0)
    )

    Y, C, O = "y", "c", "o"

    def chunk_rows(which):
        if which == C:
            return pl.ds(part, rows - 2 * part)
        side = y if which == Y else 1 - y
        return pl.ds(pl.multiple_of(side * (rows - part), 128), part)

    def chunk_id(which):
        if which == C:
            return 1
        return 2 * y if which == Y else 2 * (1 - y)

    targets = {UP: to_up, DOWN: to_down, ACROSS: to_x, OTHER: to_y, CORE: to_core}

    def w_copy(shard, which, way, own=False):
        at = chunk_rows(which)
        spot = wbuf.at[shard, at]
        return pltpu.make_async_remote_copy(
            src_ref=w_hbm.at[at] if own else spot,
            dst_ref=spot,
            send_sem=w_send.at[way, shard // 2, chunk_id(which)],
            recv_sem=w_recv.at[shard, chunk_id(which)],
            device_id=targets[way],
            device_id_type=MESH,
        )

    def shard_of(zz, xx, cc):
        return zz * 4 + xx * 2 + cc

    sent = []

    def send(cond, shard, which, way, own=False):
        def go():
            w_copy(shard, which, way, own).start()

        if cond is None:
            go()
        else:
            pl.when(cond)(go)
        sent.append((cond, shard, which, way, own))

    def both(a, b):
        return b if a is None else jnp.logical_and(a, b)

    def under(cond, go):
        if cond is None:
            go()
        else:
            pl.when(cond)(go)

    def arrive(cond, shard, which, way):
        under(cond, lambda: w_copy(shard, which, way).wait_recv())

    for which in (Y, C):
        send(has_up, r, which, UP, True)
        send(has_down, r, which, DOWN, True)
    send(None, r, Y, ACROSS, True)
    for which in (Y, C, O):
        send(None, r, which, CORE, True)

    def from_line(d, side, which):
        zz = z - d if side == UP else z + d
        ok = z >= d if side == UP else z + d < layers
        shard = shard_of(jnp.where(ok, zz, z), x, c)
        arrive(ok, shard, which, side)
        send(both(ok, has_up if side == UP else has_down), shard, which, side)
        if which == Y:
            send(ok, shard, which, ACROSS)
            send(ok, shard, which, OTHER)
        send(ok, shard, which, CORE)

    def late(d):
        for side in (UP, DOWN):
            zz = z - d if side == UP else z + d
            ok = z >= d if side == UP else z + d < layers
            send(ok, shard_of(jnp.where(ok, zz, z), x, c), C, ACROSS)

    def from_across(d, side, which):
        if d == 0:
            ok, zz = None, z
        else:
            ok = z >= d if side == UP else z + d < layers
            zz = jnp.where(ok, z - d if side == UP else z + d, z)
        shard = shard_of(zz, 1 - x, c)
        arrive(ok, shard, which, ACROSS)
        if which == Y:
            send(ok, shard, which, OTHER)
        send(ok, shard, which, CORE)

    def from_other(d, side, across):
        if d == 0:
            ok, zz = None, z
        else:
            ok = z >= d if side == UP else z + d < layers
            zz = jnp.where(ok, z - d if side == UP else z + d, z)
        shard = shard_of(zz, 1 - x if across else x, c)
        arrive(ok, shard, O, OTHER)
        send(ok, shard, O, CORE)

    def line(d, which):
        for side in (UP, DOWN):
            from_line(d, side, which)

    def across(d, which):
        for side in (UP,) if d == 0 else (UP, DOWN):
            from_across(d, side, which)

    def other(d, far_side):
        for side in (UP,) if d == 0 else (UP, DOWN):
            from_other(d, side, far_side)

    s_sent = []

    def s_copy(kind, n, src, dst, to):
        return pltpu.make_async_remote_copy(
            src_ref=src, dst_ref=dst, send_sem=s_send.at[kind, n], recv_sem=s_recv.at[kind, n],
            device_id=to, device_id_type=MESH,
        )

    def s_start(cond, *args):
        under(cond, lambda: s_copy(*args).start())
        s_sent.append((cond, args))

    def heads_at(start, n):
        return pl.ds(start, n)

    def lanes(h):
        return pl.ds(pl.multiple_of(h * head_dim, head_dim), head_dim)

    loads[0].wait()
    loads[1].wait()

    def state_loop(first):
        def step(i, _):
            for u in range(4):
                h = first + i * 4 + u
                one = lax.dot_general(
                    k[:, lanes(h)], v[:, lanes(h)], (((0,), (0,)), ((), ())),
                    preferred_element_type=jnp.float32,
                )
                st[h] = one
                st_bf[h] = one.astype(jnp.bfloat16)
            return 0

        lax.fori_loop(0, half // 4, step, 0)

    state_loop(0)
    s_start(None, ST, 0, st_bf.at[pl.ds(0, half)], b0.at[pl.ds(0, half)], to_core)
    state_loop(half)
    s_start(c == 0, ST, 1, st_bf.at[pl.ds(half, half)], b0.at[pl.ds(half, half)], to_core)

    row_of = lax.broadcasted_iota(jnp.int32, (table_rows, stretch), 0)
    onehot_t = jnp.where(row_of == idx_ref[...], 1.0, 0.0)
    onehot = jnp.transpose(onehot_t, (1, 0)).astype(jnp.bfloat16)

    def lam_step(i, _):
        for u in range(4):
            h = i * 4 + u
            full = tab_ref[:, pl.ds(h, 1), :].reshape(level_count, table_rows)
            full = jnp.transpose(full, (1, 0))
            hi = full.astype(jnp.bfloat16)
            rest = full - hi.astype(jnp.float32)
            mi = rest.astype(jnp.bfloat16)
            lo = (rest - mi.astype(jnp.float32)).astype(jnp.bfloat16)
            total = jnp.dot(onehot, lo, preferred_element_type=jnp.float32)
            total = total + jnp.dot(onehot, mi, preferred_element_type=jnp.float32)
            total = total + jnp.dot(onehot, hi, preferred_element_type=jnp.float32)
            lam[h, :, pl.ds(0, level_count)] = total
        return 0

    lax.fori_loop(0, heads // 4, lam_step, 0)

    ti = lax.broadcasted_iota(jnp.int32, (mid, mid), 0)
    si = lax.broadcasted_iota(jnp.int32, (mid, mid), 1)
    grid = jnp.zeros((mid, mid), jnp.int32)
    for bit in range(log_stretch - 1):
        grid = grid + jnp.where(
            jnp.right_shift(ti, bit) != jnp.right_shift(si, bit), 1, 0
        )
    grid = jnp.where(si <= ti, grid, -1)

    def local(first, last):
        loads_done = first == 0
        if loads_done:
            loads[2].wait()

        def step(i, _):
            for u in range(2):
                h = first + i * 2 + u
                qh, kh, vh = q[:, lanes(h)], k[:, lanes(h)], v[:, lanes(h)]
                s = lax.dot_general(
                    qh, kh, (((1,), (1,)), ((), ())), preferred_element_type=jnp.float32
                ) * scale
                weight = lam[h]

                def pick(w):
                    out = jnp.zeros((mid, mid), jnp.float32)
                    for level in range(log_stretch):
                        out = jnp.where(grid == level, w[:, level : level + 1], out)
                    return out

                low, high = weight[:mid], weight[mid:]
                p00 = (pick(low) * s[:mid, :mid]).astype(jnp.bfloat16)
                p10 = (high[:, log_stretch : log_stretch + 1] * s[mid:, :mid]).astype(jnp.bfloat16)
                p11 = (pick(high) * s[mid:, mid:]).astype(jnp.bfloat16)
                mixed[pl.ds(0, mid), lanes(h)] = jnp.dot(
                    p00, vh[:mid], preferred_element_type=jnp.float32
                )
                mixed[pl.ds(mid, mid), lanes(h)] = jnp.dot(
                    jnp.concatenate([p10, p11], axis=1), vh, preferred_element_type=jnp.float32
                )
            return 0

        lax.fori_loop(0, (last - first) // 2, step, 0)

    def far(bit, bucket):
        def step(i, _):
            for u in range(4):
                h = i * 4 + u
                term = jnp.dot(q[:, lanes(h)], bucket[h], preferred_element_type=jnp.float32)
                level = log_stretch + 1 + bit
                weight = lam[h][:, level : level + 1]
                mixed[:, lanes(h)] = mixed[:, lanes(h)] + weight * term * scale
            return 0

        lax.fori_loop(0, heads // 4, step, 0)

    def own(n):
        return pl.ds(mine + n * piece, piece)

    def chip_sum():
        pl.when(c == 0)(lambda: s_copy(ST, 0, st_bf.at[pl.ds(0, half)], b0.at[pl.ds(0, half)], to_core).wait_recv())
        pl.when(c == 1)(lambda: s_copy(ST, 1, st_bf.at[pl.ds(half, half)], b0.at[pl.ds(half, half)], to_core).wait_recv())
        for n in range(2):
            def step(i, _, n=n):
                h = n * piece + i
                one = st[mine + h] + b0[mine + h].astype(jnp.float32)
                ps[h] = one
                ps_bf[h] = one.astype(jnp.bfloat16)
                return 0

            lax.fori_loop(0, piece, step, 0)
            s_start(None, XQ, n, ps_bf.at[pl.ds(n * piece, piece)], b1.at[own(n)], to_x)

    def quad_sum():
        even = lax.rem(z, 2) == 0
        for n in range(2):
            s_copy(XQ, n, ps_bf.at[pl.ds(n * piece, piece)], b1.at[own(n)], to_x).wait_recv()
            s_start(x == 1, B1C, n, b1.at[own(n)], b1.at[own(n)], to_core)

            def step(i, _, n=n):
                h = n * piece + i
                one = ps[h] + b1[mine + h].astype(jnp.float32)
                quad[h] = one
                quad_bf[h] = one.astype(jnp.bfloat16)
                return 0

            lax.fori_loop(0, piece, step, 0)
            s_start(even, ZQ, n, quad_bf.at[pl.ds(n * piece, piece)], b2.at[own(n)], to_up)

    def layer_sum():
        odd = lax.rem(z, 2) == 1
        for n in range(2):
            at = pl.ds(n * piece, piece)
            pl.when(odd)(lambda: s_copy(ZQ, n, quad_bf.at[at], b2.at[own(n)], to_down).wait_recv())
            s_start(odd, B2C, n, b2.at[own(n)], b2.at[own(n)], to_core)

            def sums(n=n):
                def step(i, _):
                    h = n * piece + i
                    ps_bf2[h] = (quad[h] + b2[mine + h].astype(jnp.float32)).astype(jnp.bfloat16)
                    return 0

                lax.fori_loop(0, piece, step, 0)

            pl.when(z == 1)(sums)
            s_start(z == 1, ZS, n, ps_bf2.at[at], b3.at[own(n)], to_up)

    ps_bf2 = quad_bf

    def top_sum(layer):
        there = z == layer
        for n in range(2):
            def arrived(n=n):
                s_copy(ZS, n, b3.at[own(n)], b3.at[own(n)], to_down).wait_recv()

            pl.when(there)(arrived)
            if layer + 1 < layers:
                s_start(there, ZS, n, b3.at[own(n)], b3.at[own(n)], to_up)
            s_start(there, B3C, n, b3.at[own(n)], b3.at[own(n)], to_core)

    def theirs(n):
        return pl.ds(half - mine + n * piece, piece)

    def from_core(kind, buf):
        for n in range(2):
            s_copy(kind, n, buf.at[theirs(n)], buf.at[theirs(n)], to_core).wait_recv()

    def far0():
        s_copy(ST, 0, st_bf.at[pl.ds(0, half)], b0.at[pl.ds(0, half)], to_core).wait_recv()
        far(0, b0)

    def far1():
        from_core(B1C, b1)
        far(1, b1)

    def far2():
        from_core(B2C, b2)
        far(2, b2)

    def far3():
        from_core(B3C, b3)
        far(3, b3)

    def norm_step(i, _):
        for u in range(4):
            h = i * 4 + u
            m = mixed[:, lanes(h)]
            inv = lax.rsqrt(jnp.mean(m * m, axis=1, keepdims=True) + 1e-06)
            normed[:, lanes(h)] = (m * inv * gain_ref[:, lanes(h)]).astype(jnp.bfloat16)
        return 0

    def partner(column):
        def step(zz, _):
            j = zz * 2 + column
            shard = j * 2 + 1 - c
            for n, size, start in ((0, part, 0), (1, rows - 2 * part, part), (2, part, rows - part)):
                at = pl.ds(start, size)
                pltpu.make_async_remote_copy(
                    src_ref=wbuf.at[shard, at], dst_ref=wbuf.at[shard, at],
                    send_sem=w_send.at[CORE, j, n], recv_sem=w_recv.at[shard, n],
                    device_id=to_core, device_id_type=MESH,
                ).wait_recv()
            return 0

        lax.fori_loop(0, layers, step, 0)

    def project(column):
        def step(zz, _):
            j = zz * 2 + column
            both_cols = jnp.concatenate([wbuf[2 * j], wbuf[2 * j + 1]], axis=1)
            out_ref[:, pl.ds(pl.multiple_of(j * 2 * cols, 2 * cols), 2 * cols)] = jnp.dot(
                normed[...], both_cols, preferred_element_type=jnp.float32
            ).astype(jnp.bfloat16)
            return 0

        lax.fori_loop(0, layers, step, 0)

    chip_sum()
    across(0, Y)
    line(1, Y)
    local(0, 4)
    line(1, C)
    local(4, 6)
    line(2, Y)
    other(1, False)
    quad_sum()
    line(2, C)
    send(None, r, C, ACROSS, True)
    late(1)
    other(0, True)
    local(6, 8)
    line(3, Y)
    across(1, Y)
    layer_sum()
    line(3, C)
    late(2)
    late(3)
    other(2, False)
    across(2, Y)
    local(8, 12)
    top_sum(layers - 2)
    other(1, True)
    across(0, C)
    local(12, 16)
    pl.when(c == 1)(far0)
    across(1, C)
    other(3, False)
    pl.when(x == 1)(far1)
    across(3, Y)
    other(2, True)
    top_sum(layers - 1)
    pl.when(lax.rem(z, 2) == 1)(far2)
    across(2, C)
    pl.when(z >= 2)(far3)
    lax.fori_loop(0, heads // 4, norm_step, 0)
    loads[3].wait()
    partner(x)
    across(3, C)
    other(3, True)
    project(x)
    partner(1 - x)
    project(1 - x)

    for cond, shard, which, way, is_own in sent:
        under(cond, lambda: w_copy(shard, which, way, is_own).wait_send())
    for cond, args in s_sent:
        under(cond, lambda: s_copy(*args).wait_send())


def kernel_body(queries, keys, values, level_index, level_table, norm_gain, out_weight):
    stretch, width = queries.shape
    table_rows, level_count, heads = level_table.shape
    head_dim = width // heads
    rows, cols = out_weight.shape
    count = lax.axis_size("seq")
    half = heads // 2
    bf, f32 = jnp.bfloat16, jnp.float32
    part = rows * 3 // 8
    square = (head_dim, head_dim)
    any_ = pl.BlockSpec(memory_space=pl.ANY)
    vmem = pl.BlockSpec(memory_space=pltpu.VMEM)
    return pl.pallas_call(
        functools.partial(kernel, (count, 2, part)),
        out_shape=jax.ShapeDtypeStruct((stretch, width), bf),
        in_specs=[any_, any_, any_, vmem, vmem, vmem, any_],
        out_specs=vmem,
        scratch_shapes=[
            pltpu.VMEM((stretch, width), bf),
            pltpu.VMEM((stretch, width), bf),
            pltpu.VMEM((stretch, width), bf),
            pltpu.VMEM((count, rows, cols), bf),
            pltpu.VMEM((heads, *square), f32),
            pltpu.VMEM((heads, *square), bf),
            pltpu.VMEM((heads, *square), bf),
            pltpu.VMEM((heads, *square), bf),
            pltpu.VMEM((heads, *square), bf),
            pltpu.VMEM((heads, *square), bf),
            pltpu.VMEM((half, *square), f32),
            pltpu.VMEM((half, *square), bf),
            pltpu.VMEM((half, *square), f32),
            pltpu.VMEM((half, *square), bf),
            pltpu.VMEM((stretch, width), f32),
            pltpu.VMEM((stretch, width), bf),
            pltpu.VMEM((heads, stretch, 128), f32),
            pltpu.SemaphoreType.DMA((4,)),
            pltpu.SemaphoreType.DMA((5, count // 2, 3)),
            pltpu.SemaphoreType.DMA((count, 3)),
            pltpu.SemaphoreType.DMA((7, 2)),
            pltpu.SemaphoreType.DMA((7, 2)),
        ],
        compiler_params=pltpu.CompilerParams(collective_id=0, has_side_effects=True),
    )(
        queries, keys, values, level_index.reshape(1, stretch),
        jnp.transpose(level_table, (1, 2, 0)), norm_gain.reshape(1, width), out_weight,
    )


def body(queries, keys, values, level_index, level_table, norm_gain, out_weight):
    heads = level_table.shape[2]
    fits = (
        lax.axis_size("seq") == 1 << 4
        and lax.axis_size("grp") == 2
        and out_weight.shape[1] % 128 == 0
        and queries.shape[1] // heads == 128
        and heads % 4 == 0
    )
    run = kernel_body if fits else plain_body
    return run(queries, keys, values, level_index, level_table, norm_gain, out_weight)


def solution(mesh):
    placed = (
        P(("grp", "seq"), None),
        P(("grp", "seq"), None),
        P(("grp", "seq"), None),
        P(("grp", "seq")),
        P(),
        P(),
        P(None, "seq"),
    )
    return jax.shard_map(
        body, mesh=mesh, in_specs=placed, out_specs=P(("grp", "seq"), None), check_vma=False
    )
```
